32 devices in a mesh: rcv: 32 (over z, y, x, core).
Axes of the slice: x: 2, y: 2, z: 4, core: 2. Of those that a mesh axis runs over, the one named last changes fastest.
Arguments:
- predictions: bfloat16 [32768, 384], P('rcv'), may hold values from -6 to 6
- observed: bfloat16 [2, 32768, 1024], P(None, 'rcv'), may hold values from -0.3984375 to 0.3984375
- partners: int32 [2, 32], replicated, may hold values from 0 to 31, as said below
- green_block: bfloat16 [32768, 512], P('rcv'), may hold values from -0.0625 to 0.0625
Outputs:
- gradient: float32 [512, 384], P('rcv')
The draws below stay inside these ranges and needn't reach their ends.
Inputs may be any that keep to these rules, and one draw needn't show every extreme that they name: `partners`: row m pairs block b with block b XOR s_m for a meeting offset s_m; s_0 lies in 1 to 30 and s_1 = s_0 XOR (31).
All inputs are finite; a program needn't handle non-finite values.
Results may differ from the reference program's by a relative error of at most 0.0034.
Values may be sent and summed in bfloat16 or wider, within the bound.
No kernel may reach another device: no remote copies, remote signals or barrier semaphores. Data moves between devices by JAX's collectives and lax.ppermute only.
A program may use at most 64 MiB of HBM per device.

```python
import jax
import jax.numpy as jnp
from jax import lax

R_DEV = 1024
NT = 384
CELLS = 512
MEET = 2
RT = 32768
N_RCV = 32


def draw_partners(key, part):
    first = jax.random.randint(key, (), 1, N_RCV - 1).astype(jnp.int32)
    second = jnp.bitwise_xor(first, N_RCV - 1)
    blocks = jnp.arange(N_RCV, dtype=jnp.int32)
    return jnp.stack([jnp.bitwise_xor(blocks, first), jnp.bitwise_xor(blocks, second)]).astype(jnp.int32)


def spiked(array, own_key, source, target, shards_of, factor):
    def block_of(position):
        return (jnp.arange(array.shape[position]) // (array.shape[position] // shards_of)).reshape((-1,) + (1,) * (array.ndim - 1 - position))

    one_side = jax.random.permutation(own_key, shards_of)[block_of(target)]
    second = (block_of(target) + shards_of // 2) % shards_of
    return jnp.where((block_of(source) == one_side) | (block_of(source) == second), factor * array, array)


def block_scale(stream_key, extent, pieces, smallest, top_value):
    level = 1.0
    for dim, shards_of in pieces:
        steps = jax.random.uniform(jax.random.fold_in(jax.random.fold_in(stream_key, 6), dim), (shards_of,), jnp.float32, smallest / len(pieces), top_value / len(pieces))
        level = level * jnp.repeat(jnp.exp(steps), extent[dim] // shards_of).reshape((-1,) + (1,) * (len(extent) - 1 - dim))
    return level


def noise(key, shape, scale, bound, pieces=(), kind=jnp.bfloat16):
    level = block_scale(key, shape, pieces, -0.22, 0.18) if pieces else 1.0
    result = jax.random.normal(key, shape, jnp.float32) * scale * level
    return jnp.minimum(jnp.maximum(result, -bound), bound).astype(kind)


def heavy_noise(own_key, extent, spread, limit, split, heavy, kind=jnp.bfloat16):
    array = spread * jax.random.normal(own_key, extent, jnp.float32)
    if split:
        array = array * block_scale(own_key, extent, split, -0.22, 0.18)
    return jnp.clip(spiked(array, jax.random.fold_in(own_key, 3), *heavy), -limit, limit).astype(kind)


def setup_inputs(seed: int = 0) -> dict:
    keys = jax.random.split(jax.random.key(seed), 5)
    return {
        "predictions": noise(keys[0], (RT, NT), 1.0, 6.0, ((0, 32),)),
        "observed": noise(keys[1], (MEET, RT, R_DEV), 0.05, 0.3984375, ((1, 32),)),
        "partners": draw_partners(jax.random.fold_in(keys[4], 71), 0),
        "green_block": heavy_noise(keys[3], (RT, CELLS), RT ** -0.5, 0.0625, ((0, 32),), (0, 1, 32, 2.75)),
    }


student_nu = 0.01


def reference(predictions, observed, partners, green_block):
    inverse = 1.0 / NT
    blocks = predictions.reshape(N_RCV, R_DEV, NT)
    tiles = observed.reshape(MEET, N_RCV, R_DEV, R_DEV)

    def one_block(device):
        mine = lax.dynamic_index_in_dim(blocks, device, 0, keepdims=False)
        own_sum = jnp.zeros((R_DEV, NT), jnp.float32)
        backs = []
        for meeting in range(MEET):
            partner = partners[meeting, device].astype(jnp.int32)
            other = lax.dynamic_index_in_dim(blocks, partner, 0, keepdims=False)
            tile_obs = lax.dynamic_index_in_dim(tiles[meeting], device, 0, keepdims=False)
            gram_tile = lax.dot_general(mine, other, (((1,), (1,)), ((), ())), preferred_element_type=jnp.float32)
            residual = gram_tile * inverse - tile_obs.astype(jnp.float32)
            weights = ((student_nu + 1.0) * residual / (student_nu + residual * residual)).astype(jnp.bfloat16)
            own_sum = own_sum + jnp.dot(weights, other, preferred_element_type=jnp.float32) * inverse
            back_rows = lax.dot_general(weights, mine, (((0,), (0,)), ((), ())), preferred_element_type=jnp.float32) * inverse
            backs.append(back_rows.astype(jnp.bfloat16))
        return own_sum, jnp.stack(backs)

    own_all, back_all = lax.map(one_block, jnp.arange(N_RCV, dtype=jnp.int32))
    adjoint = own_all
    for meeting in range(MEET):
        adjoint = adjoint + jnp.take(back_all[:, meeting], partners[meeting].astype(jnp.int32), axis=0).astype(jnp.float32)
    adjoint = adjoint.astype(jnp.bfloat16).reshape(RT, NT)
    return lax.dot_general(green_block, adjoint, (((0,), (0,)), ((), ())), preferred_element_type=jnp.float32)
```

```python
import jax
import jax.numpy as jnp
from jax import lax
from jax.sharding import PartitionSpec as P

student_nu = 0.01
direct_bits = 5


def send(value, offset):
    if offset == 0:
        return value
    return lax.ppermute(value, "rcv", [(i, i ^ offset) for i in range(lax.axis_size("rcv"))])


def pair_tile(mine, partner_rows, tile_obs):
    inverse = 1.0 / mine.shape[1]
    gram_tile = lax.dot_general(
        mine, partner_rows, (((1,), (1,)), ((), ())), preferred_element_type=jnp.float32
    )
    residual = gram_tile * inverse - tile_obs.astype(jnp.float32)
    weights = ((student_nu + 1.0) * residual / (student_nu + residual * residual)).astype(
        jnp.bfloat16
    )
    own_part = jnp.dot(weights, partner_rows, preferred_element_type=jnp.float32) * inverse
    back_rows = (
        lax.dot_general(weights, mine, (((0,), (0,)), ((), ())), preferred_element_type=jnp.float32)
        * inverse
    )
    return (own_part, back_rows.astype(jnp.bfloat16))


def route_high(near, far, near_offset, low_bits, count_bits):
    for level in range(low_bits, count_bits):
        takes_near = near_offset >> level & 1 == 1
        moved = send(jnp.where(takes_near, near, far), 1 << level)
        near = jnp.where(takes_near, moved, near)
        far = jnp.where(takes_near, far, moved)
    return near, far


def stage_groups(count_bits):
    groups, level = [], 0
    while level < count_bits:
        width = min(1 if level == 0 else 2, count_bits - level)
        groups.append((level, width))
        level += width
    return groups


def xor_order(groups):
    order = [0]
    for level, width in groups:
        order = [block | digit << level for block in order for digit in range(1 << width)]
    return order


def scatter_sum(green_rows, adjoint, groups):
    rows = green_rows.shape[0]
    parts = []
    level, width = groups[0]
    size = rows >> width
    for digit in range(1 << width):
        parts.append(
            jnp.dot(
                green_rows[digit * size : (digit + 1) * size],
                adjoint,
                preferred_element_type=jnp.float32,
            )
        )
    total = None
    for stage, (level, width) in enumerate(groups):
        if stage > 0:
            size = total.shape[0] >> width
            parts = [total[digit * size : (digit + 1) * size] for digit in range(1 << width)]
        moved = [send(parts[digit], digit << level) for digit in range(1, 1 << width)]
        total = parts[0]
        for piece in moved:
            total = total + piece
    return total


def shards(predictions, observed, partners, green_block):
    device = lax.axis_index("rcv")
    devices = lax.axis_size("rcv")
    count_bits = devices.bit_length() - 1
    low_bits = min(direct_bits, count_bits)
    top = low_bits - 1
    mask = (1 << low_bits) - 1
    first_offset = partners[0, 0]
    first_far = first_offset >> top & 1
    near_offset = jnp.where(first_far == 1, partners[1, 0], first_offset)
    near_tile = lax.dynamic_index_in_dim(observed, first_far, 0, keepdims=False)
    far_tile = lax.dynamic_index_in_dim(observed, 1 - first_far, 0, keepdims=False)

    groups = stage_groups(count_bits)
    cells = green_block.shape[1]
    blocks = green_block.T.reshape(devices, cells // devices, green_block.shape[0])
    wanted = jnp.bitwise_xor(jnp.array(xor_order(groups), jnp.int32), device)
    green_rows = jnp.take(blocks, wanted, axis=0).reshape(cells, green_block.shape[0])

    near_in, far_in = route_high(predictions, predictions, near_offset, low_bits, count_bits)

    def branch(offset):
        def run(near_in, far_in, near_tile, far_tile, predictions):
            near_rows = send(near_in, offset)
            far_rows = send(far_in, offset ^ mask)
            near_own, near_back = pair_tile(predictions, near_rows, near_tile)
            near_return = send(near_back, offset)
            far_own, far_back = pair_tile(predictions, far_rows, far_tile)
            far_return = send(far_back, offset ^ mask)
            return near_own + far_own, near_return, far_return

        return run

    lowest = 1 if low_bits == count_bits else 0
    own, near_return, far_return = lax.switch(
        (near_offset & mask) - lowest,
        [branch(offset) for offset in range(lowest, 1 << top)],
        near_in,
        far_in,
        near_tile,
        far_tile,
        predictions,
    )
    near_return, far_return = route_high(near_return, far_return, near_offset, low_bits, count_bits)
    adjoint = (own + near_return.astype(jnp.float32) + far_return.astype(jnp.float32)).astype(
        jnp.bfloat16
    )
    return scatter_sum(green_rows, adjoint, groups)


def solution(mesh):
    placed = (P("rcv", None), P(None, "rcv", None), P(), P("rcv", None))
    return jax.shard_map(
        shards, mesh=mesh, in_specs=placed, out_specs=P("rcv", None), check_vma=False
    )
```

```python
import functools

import jax
import jax.numpy as jnp
from jax import lax
from jax.experimental import pallas as pl
from jax.experimental.pallas import tpu as pltpu
from jax.sharding import PartitionSpec as P

student_nu = 0.01
direct_bits = 5
chunk_rows = 256
f32 = jnp.float32


def send(value, offset):
    if offset == 0:
        return value
    return lax.ppermute(value, "rcv", [(i, i ^ offset) for i in range(lax.axis_size("rcv"))])


def contract_last(left, right):
    return lax.dot_general(left, right, (((1,), (1,)), ((), ())), preferred_element_type=f32)


def pair_kernel(_, mine_ref, far_ref, near_ref, obs_ref, own_ref, far_back, near_back, mine_t):
    member, chunk = pl.program_id(0), pl.program_id(1)
    inverse = 1.0 / mine_ref.shape[1]

    @pl.when((member == 0) & (chunk == 0))
    def _():
        mine_t[...] = mine_ref[...].T
        own_ref[...] = jnp.zeros_like(own_ref)

    def tile(other_ref, back_ref):
        other = other_ref[...]
        residual = contract_last(mine_ref[...], other) * inverse - obs_ref[...].astype(f32)
        weights = (student_nu + 1.0) * residual / (student_nu + residual * residual)
        weights = weights.astype(jnp.bfloat16)
        back = jnp.dot(mine_t[...], weights, preferred_element_type=f32) * inverse
        back_ref[...] = back.astype(jnp.bfloat16)
        own_ref[...] += contract_last(other.T, weights) * inverse

    pl.when(member == 0)(lambda: tile(far_ref, far_back))
    pl.when(member == 1)(lambda: tile(near_ref, near_back))


def pair_products(mine, far_rows, near_rows, observed, far_index):
    rows, samples = mine.shape
    chunks = rows // chunk_rows
    last = chunks - 1

    def far_chunk(member, chunk):
        return jnp.where(member == 0, chunk, last)

    def near_chunk(member, chunk):
        return jnp.where(member == 1, chunk, 0)

    back = jax.ShapeDtypeStruct((samples, rows), jnp.bfloat16)
    return pl.pallas_call(
        pair_kernel,
        out_shape=(jax.ShapeDtypeStruct((samples, rows), f32), back, back),
        grid_spec=pltpu.PrefetchScalarGridSpec(
            num_scalar_prefetch=1,
            grid=(2, chunks),
            in_specs=[
                pl.BlockSpec((rows, samples), lambda m, c, far: (0, 0)),
                pl.BlockSpec((chunk_rows, samples), lambda m, c, far: (far_chunk(m, c), 0)),
                pl.BlockSpec((chunk_rows, samples), lambda m, c, far: (near_chunk(m, c), 0)),
                pl.BlockSpec((None, rows, chunk_rows), lambda m, c, far: (far[0] ^ m, 0, c)),
            ],
            out_specs=[
                pl.BlockSpec((samples, rows), lambda m, c, far: (0, 0)),
                pl.BlockSpec((samples, chunk_rows), lambda m, c, far: (0, far_chunk(m, c))),
                pl.BlockSpec((samples, chunk_rows), lambda m, c, far: (0, near_chunk(m, c))),
            ],
            scratch_shapes=[pltpu.VMEM((samples, rows), jnp.bfloat16)],
        ),
        compiler_params=pltpu.CompilerParams(dimension_semantics=("arbitrary", "arbitrary")),
    )(far_index, mine, far_rows, near_rows, observed)


def partial_kernel(order, here_ref, own_ref, far_ref, near_ref, green_ref, *outs_and_scratch):
    outs, (total, turned) = outs_and_scratch[:-2], outs_and_scratch[-2:]
    chunk = pl.program_id(0)
    adjoint = own_ref[...] + far_ref[...].astype(f32) + near_ref[...].astype(f32)
    product = jnp.dot(adjoint.astype(jnp.bfloat16), green_ref[...], preferred_element_type=f32)

    @pl.when(chunk == 0)
    def _():
        total[...] = product

    @pl.when(chunk > 0)
    def _():
        total[...] += product

    @pl.when(chunk == pl.num_programs(0) - 1)
    def _():
        turned[...] = total[...].T
        block = turned.shape[0] // len(order)
        each = len(order) // len(outs)
        for place, index in enumerate(order):
            source = pl.multiple_of((here_ref[0] ^ index) * block, block)
            spot = place % each * block
            outs[place // each][spot : spot + block, :] = turned[pl.ds(source, block), :]


def partial_gradient(here, own, far_return, near_return, green_block, order, parts):
    samples, rows = own.shape
    cells = green_block.shape[1]
    natural = cells // len(order) % 8 != 0
    kernel_order, kernel_parts = ([0], 1) if natural else (order, parts)
    column = pl.BlockSpec((samples, chunk_rows), lambda c, here: (0, c))
    size = cells // kernel_parts
    outs = pl.pallas_call(
        functools.partial(partial_kernel, kernel_order),
        out_shape=[jax.ShapeDtypeStruct((size, samples), f32)] * kernel_parts,
        grid_spec=pltpu.PrefetchScalarGridSpec(
            num_scalar_prefetch=1,
            grid=(rows // chunk_rows,),
            in_specs=[column] * 3 + [pl.BlockSpec((chunk_rows, cells), lambda c, here: (c, 0))],
            out_specs=[pl.BlockSpec((size, samples), lambda c, here: (0, 0))] * kernel_parts,
            scratch_shapes=[pltpu.VMEM((samples, cells), f32), pltpu.VMEM((cells, samples), f32)],
        ),
        compiler_params=pltpu.CompilerParams(dimension_semantics=("arbitrary",)),
    )(here * 0 if natural else here, own, far_return, near_return, green_block)
    if natural:
        blocks = outs[0].reshape(len(order), cells // len(order), samples)
        wanted = jnp.bitwise_xor(jnp.array(order, jnp.int32), here)
        blocks = jnp.take(blocks, wanted, axis=0).reshape(parts, cells // parts, samples)
        outs = [blocks[part] for part in range(parts)]
    return list(outs)


def route_high(near, far, near_offset, low_bits, count_bits):
    for level in range(low_bits, count_bits):
        takes_near = near_offset >> level & 1 == 1
        moved = send(jnp.where(takes_near, near, far), 1 << level)
        near = jnp.where(takes_near, moved, near)
        far = jnp.where(takes_near, far, moved)
    return near, far


def route_low(near, far, near_offset, low_bits, count_bits):
    mask = (1 << low_bits) - 1
    lowest = 1 if low_bits == count_bits else 0

    def branch(offset):
        def run(near, far):
            far_moved = send(far, offset ^ mask)
            return send(near, offset), far_moved

        return run

    branches = [branch(offset) for offset in range(lowest, 1 << low_bits - 1)]
    return lax.switch((near_offset & mask) - lowest, branches, near, far)


def stage_groups(count_bits):
    groups, level = [], 0
    while level < count_bits:
        width = min(1 if level == 0 else 2, count_bits - level)
        groups.append((level, width))
        level += width
    return groups


def xor_order(groups):
    order = [0]
    for level, width in groups:
        order = [block | digit << level for block in order for digit in range(1 << width)]
    return order


def scatter_sum(parts, groups):
    total = None
    for level, width in groups:
        if total is not None:
            size = total.shape[0] >> width
            parts = [total[digit * size : (digit + 1) * size] for digit in range(1 << width)]
        moved = [send(parts[digit], digit << level) for digit in range(1, 1 << width)]
        total = parts[0]
        for piece in moved:
            total = total + piece
    return total


def shards(predictions, observed, partners, green_block):
    count_bits = lax.axis_size("rcv").bit_length() - 1
    low_bits = min(direct_bits, count_bits)
    here = lax.axis_index("rcv").astype(jnp.int32).reshape(1)
    first_offset = partners[0, 0]
    first_far = first_offset >> low_bits - 1 & 1
    near_offset = jnp.where(first_far == 1, partners[1, 0], first_offset)
    far_index = (1 - first_far).reshape(1)

    near_rows, far_rows = route_high(predictions, predictions, near_offset, low_bits, count_bits)
    near_rows, far_rows = route_low(near_rows, far_rows, near_offset, low_bits, count_bits)
    own, far_back, near_back = pair_products(
        predictions, far_rows, near_rows, observed, far_index
    )
    near_return, far_return = route_low(near_back, far_back, near_offset, low_bits, count_bits)
    near_return, far_return = route_high(near_return, far_return, near_offset, low_bits, count_bits)

    groups = stage_groups(count_bits)
    parts = partial_gradient(
        here, own, far_return, near_return, green_block, xor_order(groups), 1 << groups[0][1]
    )
    return scatter_sum(parts, groups)


def solution(mesh):
    placed = (P("rcv", None), P(None, "rcv", None), P(), P("rcv", None))
    return jax.shard_map(
        shards, mesh=mesh, in_specs=placed, out_specs=P("rcv", None), check_vma=False
    )
```

```python
import functools

import jax
import jax.numpy as jnp
from jax import lax
from jax.experimental import pallas as pl
from jax.experimental.pallas import tpu as pltpu
from jax.sharding import PartitionSpec as P

student_nu = 0.01
direct_bits = 5
chunk_rows = 256
turn_rows = 128
f32 = jnp.float32


def send(value, offset):
    if offset == 0:
        return value
    return lax.ppermute(value, "rcv", [(i, i ^ offset) for i in range(lax.axis_size("rcv"))])


def contract_last(left, right):
    return lax.dot_general(left, right, (((1,), (1,)), ((), ())), preferred_element_type=f32)


def turn_kernel(rows_ref, turned_ref):
    turned_ref[...] = rows_ref[...].T


def turn(value):
    rows, samples = value.shape
    return pl.pallas_call(
        turn_kernel,
        out_shape=jax.ShapeDtypeStruct((samples, rows), value.dtype),
        grid=(rows // turn_rows,),
        in_specs=[pl.BlockSpec((turn_rows, samples), lambda c: (c, 0))],
        out_specs=pl.BlockSpec((samples, turn_rows), lambda c: (0, c)),
        compiler_params=pltpu.CompilerParams(dimension_semantics=("arbitrary",)),
    )(value)


def weights_of(gram, tile_obs, samples):
    residual = gram - tile_obs.astype(f32) * samples
    weights = ((student_nu + 1.0) * samples) * residual
    weights = weights / (student_nu * samples * samples + residual * residual)
    return weights.astype(jnp.bfloat16)


def pair_kernel(
    far_steps, _, mine_ref, mine_t, far_ref, near_ref, odd_obs, even_obs,
    far_back, near_back, even_weights, odd_weights, odd_gram, held_weights,
):
    step = pl.program_id(0)
    samples = mine_ref.shape[1]
    rows = jnp.where(step < far_steps, far_ref[...], near_ref[...])
    back_even = jnp.dot(mine_t[...], held_weights[...], preferred_element_type=f32)
    odd = weights_of(odd_gram[...], odd_obs[...], samples)
    even_gram = contract_last(mine_ref[...], rows[:chunk_rows])
    odd_weights[...] = odd
    back_odd = jnp.dot(mine_t[...], odd, preferred_element_type=f32)
    even = weights_of(even_gram, even_obs[...], samples)
    even_weights[...] = even
    held_weights[...] = even
    odd_gram[...] = contract_last(mine_ref[...], rows[chunk_rows:])
    back_even = (back_even * (1.0 / samples)).astype(jnp.bfloat16)
    back_odd = (back_odd * (1.0 / samples)).astype(jnp.bfloat16)

    @pl.when(step <= far_steps)
    def _():
        far_back[:, :chunk_rows] = back_even
        far_back[:, chunk_rows:] = back_odd

    @pl.when(step > far_steps)
    def _():
        near_back[:, :chunk_rows] = back_even
        near_back[:, chunk_rows:] = back_odd


def pair_products(mine, mine_t, far_rows, near_rows, observed, far_index):
    rows, samples = mine.shape
    chunks = rows // chunk_rows
    steps = rows // (2 * chunk_rows)
    double = 2 * chunk_rows

    def rows_at(first):
        return lambda s, far: (jnp.clip(s - first, 0, steps - 1), 0)

    def back_at(first):
        return lambda s, far: (0, jnp.clip(s - first, 0, steps - 1))

    def observed_at(shift):
        def at(s, far):
            chunk = jnp.clip(2 * s + shift, 0, 2 * chunks - 1)
            later = chunk >= chunks
            return jnp.where(later, 1 - far[0], far[0]), 0, jnp.where(later, chunk - chunks, chunk)

        return at

    tile = (None, rows, chunk_rows)
    back = jax.ShapeDtypeStruct((samples, rows), jnp.bfloat16)
    weights = jax.ShapeDtypeStruct((rows, (2 * steps + 1) * chunk_rows), jnp.bfloat16)
    return pl.pallas_call(
        functools.partial(pair_kernel, steps),
        out_shape=(back, back, weights, weights),
        grid_spec=pltpu.PrefetchScalarGridSpec(
            num_scalar_prefetch=1,
            grid=(2 * steps + 1,),
            in_specs=[
                pl.BlockSpec((rows, samples), lambda s, far: (0, 0)),
                pl.BlockSpec((samples, rows), lambda s, far: (0, 0)),
                pl.BlockSpec((double, samples), rows_at(0)),
                pl.BlockSpec((double, samples), rows_at(steps)),
                pl.BlockSpec(tile, observed_at(-1)),
                pl.BlockSpec(tile, observed_at(0)),
            ],
            out_specs=[
                pl.BlockSpec((samples, double), back_at(1)),
                pl.BlockSpec((samples, double), back_at(steps + 1)),
                pl.BlockSpec((rows, chunk_rows), lambda s, far: (0, s)),
                pl.BlockSpec((rows, chunk_rows), lambda s, far: (0, s)),
            ],
            scratch_shapes=[
                pltpu.VMEM((rows, chunk_rows), f32),
                pltpu.VMEM((rows, chunk_rows), jnp.bfloat16),
            ],
        ),
        compiler_params=pltpu.CompilerParams(dimension_semantics=("arbitrary",)),
    )(far_index, mine, mine_t, far_rows, near_rows, observed, observed)


def own_kernel(far_steps, far_ref, near_ref, even_weights, odd_weights, own_ref, total):
    step = pl.program_id(1)
    rows = jnp.where(step < far_steps, far_ref[...], near_ref[...])
    own = jnp.dot(even_weights[...], rows[:chunk_rows], preferred_element_type=f32)
    own += jnp.dot(odd_weights[...], rows[chunk_rows:], preferred_element_type=f32)
    total[...] = jnp.where(step == 0, own, total[...] + own)

    @pl.when(step == pl.num_programs(1) - 1)
    def _():
        own_ref[...] = (total[...] * (1.0 / far_ref.shape[1])).T


def own_product(far, near, even_weights, odd_weights):
    rows, samples = far.shape
    steps = rows // (2 * chunk_rows)
    double = 2 * chunk_rows
    return pl.pallas_call(
        functools.partial(own_kernel, steps),
        out_shape=jax.ShapeDtypeStruct((samples, rows), f32),
        grid=(rows // chunk_rows, 2 * steps),
        in_specs=[
            pl.BlockSpec((double, samples), lambda c, s: (jnp.clip(s, 0, steps - 1), 0)),
            pl.BlockSpec((double, samples), lambda c, s: (jnp.clip(s - steps, 0, steps - 1), 0)),
            pl.BlockSpec((chunk_rows, chunk_rows), lambda c, s: (c, s)),
            pl.BlockSpec((chunk_rows, chunk_rows), lambda c, s: (c, s + 1)),
        ],
        out_specs=pl.BlockSpec((samples, chunk_rows), lambda c, s: (0, c)),
        scratch_shapes=[pltpu.VMEM((chunk_rows, samples), f32)],
        compiler_params=pltpu.CompilerParams(dimension_semantics=("arbitrary", "arbitrary")),
    )(far, near, even_weights, odd_weights)


def partial_kernel(order, here_ref, own_ref, far_ref, near_ref, green_ref, *outs_and_scratch):
    outs, (total, turned) = outs_and_scratch[:-2], outs_and_scratch[-2:]
    chunk = pl.program_id(0)
    adjoint = own_ref[...] + far_ref[...].astype(f32) + near_ref[...].astype(f32)
    product = jnp.dot(adjoint.astype(jnp.bfloat16), green_ref[...], preferred_element_type=f32)

    @pl.when(chunk == 0)
    def _():
        total[...] = product

    @pl.when(chunk > 0)
    def _():
        total[...] += product

    @pl.when(chunk == pl.num_programs(0) - 1)
    def _():
        turned[...] = total[...].T
        block = turned.shape[0] // len(order)
        each = len(order) // len(outs)
        for place, index in enumerate(order):
            source = pl.multiple_of((here_ref[0] ^ index) * block, block)
            spot = place % each * block
            outs[place // each][spot : spot + block, :] = turned[pl.ds(source, block), :]


def partial_gradient(here, own, far_return, near_return, green_block, order, parts):
    samples, rows = own.shape
    cells = green_block.shape[1]
    natural = cells // len(order) % 8 != 0
    kernel_order, kernel_parts = ([0], 1) if natural else (order, parts)
    column = pl.BlockSpec((samples, chunk_rows), lambda c, here: (0, c))
    size = cells // kernel_parts
    outs = pl.pallas_call(
        functools.partial(partial_kernel, kernel_order),
        out_shape=[jax.ShapeDtypeStruct((size, samples), f32)] * kernel_parts,
        grid_spec=pltpu.PrefetchScalarGridSpec(
            num_scalar_prefetch=1,
            grid=(rows // chunk_rows,),
            in_specs=[column] * 3 + [pl.BlockSpec((chunk_rows, cells), lambda c, here: (c, 0))],
            out_specs=[pl.BlockSpec((size, samples), lambda c, here: (0, 0))] * kernel_parts,
            scratch_shapes=[pltpu.VMEM((samples, cells), f32), pltpu.VMEM((cells, samples), f32)],
        ),
        compiler_params=pltpu.CompilerParams(dimension_semantics=("arbitrary",)),
    )(here * 0 if natural else here, own, far_return, near_return, green_block)
    if natural:
        blocks = outs[0].reshape(len(order), cells // len(order), samples)
        wanted = jnp.bitwise_xor(jnp.array(order, jnp.int32), here)
        blocks = jnp.take(blocks, wanted, axis=0).reshape(parts, cells // parts, samples)
        outs = [blocks[part] for part in range(parts)]
    return list(outs)


def route_high(near, far, near_offset, low_bits, count_bits):
    for level in range(low_bits, count_bits):
        takes_near = near_offset >> level & 1 == 1
        moved = send(jnp.where(takes_near, near, far), 1 << level)
        near = jnp.where(takes_near, moved, near)
        far = jnp.where(takes_near, far, moved)
    return near, far


def meet_both(near, far, mine, observed, near_offset, far_index, low_bits, count_bits):
    mask = (1 << low_bits) - 1
    lowest = 1 if low_bits == count_bits else 0
    offsets = range(lowest, 1 << low_bits - 1)

    def arrive(offset):
        def run(near, far, mine):
            far_rows = send(far, offset ^ mask)
            return far_rows, send(near, offset), turn(mine)

        return run

    def leave(offset):
        def run(far_rows, near_rows, far_back, near_back, *weights):
            far_return = send(far_back, offset ^ mask)
            near_return = send(near_back, offset)
            return own_product(far_rows, near_rows, *weights), far_return, near_return

        return run

    chosen = (near_offset & mask) - lowest
    far_rows, near_rows, mine_t = lax.switch(
        chosen, [arrive(offset) for offset in offsets], near, far, mine
    )
    products = pair_products(mine, mine_t, far_rows, near_rows, observed, far_index)
    return lax.switch(
        chosen, [leave(offset) for offset in offsets], far_rows, near_rows, *products
    )


def stage_groups(count_bits):
    groups, level = [], 0
    while level < count_bits:
        width = min(1 if level == 0 else 2, count_bits - level)
        groups.append((level, width))
        level += width
    return groups


def xor_order(groups):
    order = [0]
    for level, width in groups:
        order = [block | digit << level for block in order for digit in range(1 << width)]
    return order


def scatter_sum(parts, groups):
    total = None
    for level, width in groups:
        if total is not None:
            size = total.shape[0] >> width
            parts = [total[digit * size : (digit + 1) * size] for digit in range(1 << width)]
        moved = [send(parts[digit], digit << level) for digit in range(1, 1 << width)]
        total = parts[0]
        for piece in moved:
            total = total + piece
    return total


def shards(predictions, observed, partners, green_block):
    count_bits = lax.axis_size("rcv").bit_length() - 1
    low_bits = min(direct_bits, count_bits)
    here = lax.axis_index("rcv").astype(jnp.int32).reshape(1)
    first_offset = partners[0, 0]
    first_far = first_offset >> low_bits - 1 & 1
    near_offset = jnp.where(first_far == 1, partners[1, 0], first_offset)
    far_index = (1 - first_far).reshape(1)

    near_in, far_in = route_high(predictions, predictions, near_offset, low_bits, count_bits)
    own, far_return, near_return = meet_both(
        near_in, far_in, predictions, observed, near_offset, far_index, low_bits, count_bits
    )
    near_return, far_return = route_high(near_return, far_return, near_offset, low_bits, count_bits)

    groups = stage_groups(count_bits)
    parts = partial_gradient(
        here, own, far_return, near_return, green_block, xor_order(groups), 1 << groups[0][1]
    )
    return scatter_sum(parts, groups)


def solution(mesh):
    placed = (P("rcv", None), P(None, "rcv", None), P(), P("rcv", None))
    return jax.shard_map(
        shards, mesh=mesh, in_specs=placed, out_specs=P("rcv", None), check_vma=False
    )
```

```python
import functools

import jax
import jax.numpy as jnp
from jax import lax
from jax.experimental import pallas as pl
from jax.experimental.pallas import tpu as pltpu
from jax.sharding import PartitionSpec as P

student_nu = 0.01
direct_bits = 5
chunk_rows = 256
block_rows = 1024
turn_rows = 128
f32 = jnp.float32


def send(value, offset):
    if offset == 0:
        return value
    return lax.ppermute(value, "rcv", [(i, i ^ offset) for i in range(lax.axis_size("rcv"))])


def is_mixed(device, top):
    return (device >> top ^ device >> top - 1) & 1 == 1


def send_mixed(value, mixed_offset, other_offset, top):
    pairs = [
        (i, i ^ (mixed_offset if is_mixed(i, top) else other_offset))
        for i in range(lax.axis_size("rcv"))
    ]
    return lax.ppermute(value, "rcv", pairs)


def contract_last(left, right):
    return lax.dot_general(left, right, (((1,), (1,)), ((), ())), preferred_element_type=f32)


def turn_kernel(rows_ref, turned_ref):
    turned_ref[...] = rows_ref[...].T


def turn(value):
    rows, samples = value.shape
    return pl.pallas_call(
        turn_kernel,
        out_shape=jax.ShapeDtypeStruct((samples, rows), value.dtype),
        grid=(rows // turn_rows,),
        in_specs=[pl.BlockSpec((turn_rows, samples), lambda c: (c, 0))],
        out_specs=pl.BlockSpec((samples, turn_rows), lambda c: (0, c)),
        compiler_params=pltpu.CompilerParams(dimension_semantics=("arbitrary",)),
    )(value)


def weights_of(gram, tile_obs, samples):
    residual = gram - tile_obs.astype(f32) * samples
    weights = ((student_nu + 1.0) * samples) * residual
    weights = weights / (student_nu * samples * samples + residual * residual)
    return weights.astype(jnp.bfloat16)


def pair_kernel(
    far_steps, _, mine_ref, mine_t, far_ref, near_ref, odd_obs, even_obs,
    far_back, near_back, even_weights, odd_weights, odd_gram, held_weights,
):
    step = pl.program_id(0)
    samples = mine_ref.shape[1]
    rows = jnp.where(step < far_steps, far_ref[...], near_ref[...])
    back_even = jnp.dot(mine_t[...], held_weights[...], preferred_element_type=f32)
    odd = weights_of(odd_gram[...], odd_obs[...], samples)
    even_gram = contract_last(mine_ref[...], rows[:chunk_rows])
    odd_weights[...] = odd
    back_odd = jnp.dot(mine_t[...], odd, preferred_element_type=f32)
    even = weights_of(even_gram, even_obs[...], samples)
    even_weights[...] = even
    held_weights[...] = even
    odd_gram[...] = contract_last(mine_ref[...], rows[chunk_rows:])
    back_even = (back_even * (1.0 / samples)).astype(jnp.bfloat16)
    back_odd = (back_odd * (1.0 / samples)).astype(jnp.bfloat16)

    @pl.when(step <= far_steps)
    def _():
        far_back[:, :chunk_rows] = back_even
        far_back[:, chunk_rows:] = back_odd

    @pl.when(step > far_steps)
    def _():
        near_back[:, :chunk_rows] = back_even
        near_back[:, chunk_rows:] = back_odd


def pair_products(mine, mine_t, far_rows, near_rows, observed, far_index):
    rows, samples = mine.shape
    chunks = rows // chunk_rows
    steps = rows // (2 * chunk_rows)
    double = 2 * chunk_rows

    def rows_at(first):
        return lambda s, far: (jnp.clip(s - first, 0, steps - 1), 0)

    def back_at(first):
        return lambda s, far: (0, jnp.clip(s - first, 0, steps - 1))

    def observed_at(shift):
        def at(s, far):
            chunk = jnp.clip(2 * s + shift, 0, 2 * chunks - 1)
            later = chunk >= chunks
            return jnp.where(later, 1 - far[0], far[0]), 0, jnp.where(later, chunk - chunks, chunk)

        return at

    tile = (None, rows, chunk_rows)
    back = jax.ShapeDtypeStruct((samples, rows), jnp.bfloat16)
    weights = jax.ShapeDtypeStruct((rows, (2 * steps + 1) * chunk_rows), jnp.bfloat16)
    return pl.pallas_call(
        functools.partial(pair_kernel, steps),
        out_shape=(back, back, weights, weights),
        grid_spec=pltpu.PrefetchScalarGridSpec(
            num_scalar_prefetch=1,
            grid=(2 * steps + 1,),
            in_specs=[
                pl.BlockSpec((rows, samples), lambda s, far: (0, 0)),
                pl.BlockSpec((samples, rows), lambda s, far: (0, 0)),
                pl.BlockSpec((double, samples), rows_at(0)),
                pl.BlockSpec((double, samples), rows_at(steps)),
                pl.BlockSpec(tile, observed_at(-1)),
                pl.BlockSpec(tile, observed_at(0)),
            ],
            out_specs=[
                pl.BlockSpec((samples, double), back_at(1)),
                pl.BlockSpec((samples, double), back_at(steps + 1)),
                pl.BlockSpec((rows, chunk_rows), lambda s, far: (0, s)),
                pl.BlockSpec((rows, chunk_rows), lambda s, far: (0, s)),
            ],
            scratch_shapes=[
                pltpu.VMEM((rows, chunk_rows), f32),
                pltpu.VMEM((rows, chunk_rows), jnp.bfloat16),
            ],
        ),
        compiler_params=pltpu.CompilerParams(dimension_semantics=("arbitrary",)),
    )(far_index, mine, mine_t, far_rows, near_rows, observed, observed)


def own_kernel(far_steps, far_ref, near_ref, even_weights, odd_weights, own_ref, total):
    step = pl.program_id(1)
    rows = jnp.where(step < far_steps, far_ref[...], near_ref[...])
    own = jnp.dot(even_weights[...], rows[:chunk_rows], preferred_element_type=f32)
    own += jnp.dot(odd_weights[...], rows[chunk_rows:], preferred_element_type=f32)
    total[...] = jnp.where(step == 0, own, total[...] + own)

    @pl.when(step == pl.num_programs(1) - 1)
    def _():
        own_ref[...] = (total[...] * (1.0 / far_ref.shape[1])).T


def own_product(far, near, even_weights, odd_weights):
    rows, samples = far.shape
    steps = rows // (2 * chunk_rows)
    double = 2 * chunk_rows
    return pl.pallas_call(
        functools.partial(own_kernel, steps),
        out_shape=jax.ShapeDtypeStruct((samples, rows), f32),
        grid=(rows // chunk_rows, 2 * steps),
        in_specs=[
            pl.BlockSpec((double, samples), lambda c, s: (jnp.clip(s, 0, steps - 1), 0)),
            pl.BlockSpec((double, samples), lambda c, s: (jnp.clip(s - steps, 0, steps - 1), 0)),
            pl.BlockSpec((chunk_rows, chunk_rows), lambda c, s: (c, s)),
            pl.BlockSpec((chunk_rows, chunk_rows), lambda c, s: (c, s + 1)),
        ],
        out_specs=pl.BlockSpec((samples, chunk_rows), lambda c, s: (0, c)),
        scratch_shapes=[pltpu.VMEM((chunk_rows, samples), f32)],
        compiler_params=pltpu.CompilerParams(dimension_semantics=("arbitrary", "arbitrary")),
    )(far, near, even_weights, odd_weights)


def partial_kernel(order, here_ref, own_ref, far_ref, near_ref, green_ref, *outs_and_scratch):
    outs, (total, turned) = outs_and_scratch[:-2], outs_and_scratch[-2:]
    chunk = pl.program_id(0)
    adjoint = own_ref[...] + far_ref[...].astype(f32) + near_ref[...].astype(f32)
    product = jnp.dot(adjoint.astype(jnp.bfloat16), green_ref[...], preferred_element_type=f32)

    @pl.when(chunk == 0)
    def _():
        total[...] = product

    @pl.when(chunk > 0)
    def _():
        total[...] += product

    @pl.when(chunk == pl.num_programs(0) - 1)
    def _():
        turned[...] = total[...].T
        block = turned.shape[0] // len(order)
        each = len(order) // len(outs)
        for place, index in enumerate(order):
            source = pl.multiple_of((here_ref[0] ^ index) * block, block)
            spot = place % each * block
            outs[place // each][spot : spot + block, :] = turned[pl.ds(source, block), :]


def partial_gradient(here, own, far_return, near_return, green_block, order, parts):
    samples, rows = own.shape
    cells = green_block.shape[1]
    natural = cells // len(order) % 8 != 0
    kernel_order, kernel_parts = ([0], 1) if natural else (order, parts)
    column = pl.BlockSpec((samples, chunk_rows), lambda c, here: (0, c))
    size = cells // kernel_parts
    outs = pl.pallas_call(
        functools.partial(partial_kernel, kernel_order),
        out_shape=[jax.ShapeDtypeStruct((size, samples), f32)] * kernel_parts,
        grid_spec=pltpu.PrefetchScalarGridSpec(
            num_scalar_prefetch=1,
            grid=(rows // chunk_rows,),
            in_specs=[column] * 3 + [pl.BlockSpec((chunk_rows, cells), lambda c, here: (c, 0))],
            out_specs=[pl.BlockSpec((size, samples), lambda c, here: (0, 0))] * kernel_parts,
            scratch_shapes=[pltpu.VMEM((samples, cells), f32), pltpu.VMEM((cells, samples), f32)],
        ),
        compiler_params=pltpu.CompilerParams(dimension_semantics=("arbitrary",)),
    )(here * 0 if natural else here, own, far_return, near_return, green_block)
    if natural:
        blocks = outs[0].reshape(len(order), cells // len(order), samples)
        wanted = jnp.bitwise_xor(jnp.array(order, jnp.int32), here)
        blocks = jnp.take(blocks, wanted, axis=0).reshape(parts, cells // parts, samples)
        outs = [blocks[part] for part in range(parts)]
    return list(outs)


def route_high(near, far, near_offset, low_bits, count_bits):
    for level in range(low_bits, count_bits):
        takes_near = near_offset >> level & 1 == 1
        moved = send(jnp.where(takes_near, near, far), 1 << level)
        near = jnp.where(takes_near, moved, near)
        far = jnp.where(takes_near, far, moved)
    return near, far


def back_kernel(_, mine_ref, mine_t, other_ref, obs_ref, back_ref, weights_ref, *scratch):
    block, last = pl.program_id(1), pl.num_programs(1) - 1
    samples = mine_ref.shape[1]
    gram = contract_last(mine_ref[...], other_ref[...])
    weights = weights_of(gram, obs_ref[...], samples)
    weights_ref[...] = weights
    back = jnp.dot(mine_t[...], weights, preferred_element_type=f32)
    if not scratch:
        back_ref[...] = (back * (1.0 / samples)).astype(jnp.bfloat16)
        return
    (total,) = scratch
    back = jnp.where(block == 0, back, total[...] + back)
    total[...] = back

    @pl.when(block == last)
    def _():
        back_ref[...] = (back * (1.0 / samples)).astype(jnp.bfloat16)


def back_product(mine, mine_t, other, observed, meeting):
    rows, samples = mine.shape
    blocks = rows // block_rows
    return pl.pallas_call(
        back_kernel,
        out_shape=(
            jax.ShapeDtypeStruct((samples, rows), jnp.bfloat16),
            jax.ShapeDtypeStruct((rows, rows), jnp.bfloat16),
        ),
        grid_spec=pltpu.PrefetchScalarGridSpec(
            num_scalar_prefetch=1,
            grid=(rows // chunk_rows, blocks),
            in_specs=[
                pl.BlockSpec((block_rows, samples), lambda c, r, meeting: (r, 0)),
                pl.BlockSpec((samples, block_rows), lambda c, r, meeting: (0, r)),
                pl.BlockSpec((chunk_rows, samples), lambda c, r, meeting: (c, 0)),
                pl.BlockSpec(
                    (None, block_rows, chunk_rows), lambda c, r, meeting: (meeting[0], r, c)
                ),
            ],
            out_specs=[
                pl.BlockSpec((samples, chunk_rows), lambda c, r, meeting: (0, c)),
                pl.BlockSpec((block_rows, chunk_rows), lambda c, r, meeting: (r, c)),
            ],
            scratch_shapes=[pltpu.VMEM((samples, chunk_rows), f32)] if blocks > 1 else [],
        ),
        compiler_params=pltpu.CompilerParams(dimension_semantics=("arbitrary", "arbitrary")),
    )(meeting, mine, mine_t, other, observed)


def total_kernel(first_ref, second_ref, first_weights, second_weights, own_ref, total):
    step = pl.program_id(1)
    own = jnp.dot(first_weights[...], first_ref[...], preferred_element_type=f32)
    own += jnp.dot(second_weights[...], second_ref[...], preferred_element_type=f32)
    total[...] = jnp.where(step == 0, own, total[...] + own)

    @pl.when(step == pl.num_programs(1) - 1)
    def _():
        own_ref[...] = (total[...] * (1.0 / first_ref.shape[1])).T


def own_total(first, second, first_weights, second_weights):
    rows, samples = first.shape
    values = pl.BlockSpec((chunk_rows, samples), lambda c, s: (s, 0))
    weights = pl.BlockSpec((chunk_rows, chunk_rows), lambda c, s: (c, s))
    return pl.pallas_call(
        total_kernel,
        out_shape=jax.ShapeDtypeStruct((samples, rows), f32),
        grid=(rows // chunk_rows, rows // chunk_rows),
        in_specs=[values, values, weights, weights],
        out_specs=pl.BlockSpec((samples, chunk_rows), lambda c, s: (0, c)),
        scratch_shapes=[pltpu.VMEM((chunk_rows, samples), f32)],
        compiler_params=pltpu.CompilerParams(dimension_semantics=("arbitrary", "arbitrary")),
    )(first, second, first_weights, second_weights)


def meet_apart(near, far, mine, observed, far_index, low_offset, low_bits, lowest):
    mask = (1 << low_bits) - 1
    offsets = range(lowest, 1 << low_bits - 2)

    def arrive(offset):
        def run(near, far, mine):
            far_rows = send(far, offset ^ mask)
            return far_rows, send(near, offset), turn(mine)

        return run

    def leave(offset):
        def run(far_rows, near_rows, far_back, near_back, *weights):
            far_return = send(far_back, offset ^ mask)
            near_return = send(near_back, offset)
            return own_product(far_rows, near_rows, *weights), far_return, near_return

        return run

    chosen = low_offset - lowest
    far_rows, near_rows, mine_t = lax.switch(
        chosen, [arrive(offset) for offset in offsets], near, far, mine
    )
    products = pair_products(mine, mine_t, far_rows, near_rows, observed, far_index)
    return lax.switch(
        chosen, [leave(offset) for offset in offsets], far_rows, near_rows, *products
    )


def meet_mixed(near, far, mine, observed, far_index, low_offset, low_bits):
    mask = (1 << low_bits) - 1
    top = low_bits - 1
    lowest = 1 << top - 1
    mixed = is_mixed(lax.axis_index("rcv"), top)

    def branch(offset):
        close, apart = offset, offset ^ mask

        def run(near, far, mine, observed, first_meeting):
            first_out = near if near is far else jnp.where(mixed, near, far)
            second_out = near if near is far else jnp.where(mixed, far, near)
            first = send_mixed(first_out, close, apart, top)
            second = send_mixed(second_out, apart, close, top)
            mine_t = turn(mine)
            back, first_weights = back_product(mine, mine_t, first, observed, first_meeting)
            first_return = send_mixed(back, apart, close, top)
            back, second_weights = back_product(mine, mine_t, second, observed, 1 - first_meeting)
            second_return = send_mixed(back, close, apart, top)
            own = own_total(first, second, first_weights, second_weights)
            return own, first_return, second_return

        return run

    first_meeting = jnp.where(mixed, far_index, 1 - far_index)
    if near is far:
        one = lambda run: lambda rows, *rest: run(rows, rows, *rest)
        branches = [one(branch(offset)) for offset in range(lowest, 1 << top)]
        return lax.switch(low_offset - lowest, branches, near, mine, observed, first_meeting)
    branches = [branch(offset) for offset in range(lowest, 1 << top)]
    own, first_return, second_return = lax.switch(
        low_offset - lowest, branches, near, far, mine, observed, first_meeting
    )
    return (
        own,
        jnp.where(mixed, second_return, first_return),
        jnp.where(mixed, first_return, second_return),
    )


def meet_both(near, far, mine, observed, near_offset, far_index, low_bits, count_bits):
    low_offset = near_offset & (1 << low_bits) - 1
    lowest = 1 if low_bits == count_bits else 0

    def with_inputs(meet, *more):
        if near is far:
            return lambda rows, *rest: meet(rows, rows, *rest, *more)
        return lambda near, far, *rest: meet(near, far, *rest, *more)

    inputs = (near,) if near is far else (near, far)
    return lax.cond(
        low_offset >> low_bits - 2 & 1 == 1,
        with_inputs(meet_mixed, low_bits),
        with_inputs(meet_apart, low_bits, lowest),
        *inputs,
        mine,
        observed,
        far_index,
        low_offset,
    )


def stage_groups(count_bits):
    groups, level = [], 0
    while level < count_bits:
        width = min(1 if level == 0 else 2, count_bits - level)
        groups.append((level, width))
        level += width
    return groups


def xor_order(groups):
    order = [0]
    for level, width in groups:
        order = [block | digit << level for block in order for digit in range(1 << width)]
    return order


def scatter_sum(parts, groups):
    total = None
    for level, width in groups:
        if total is not None:
            size = total.shape[0] >> width
            parts = [total[digit * size : (digit + 1) * size] for digit in range(1 << width)]
        moved = [send(parts[digit], digit << level) for digit in range(1, 1 << width)]
        total = parts[0]
        for piece in moved:
            total = total + piece
    return total


def shards(predictions, observed, partners, green_block):
    count_bits = lax.axis_size("rcv").bit_length() - 1
    low_bits = min(direct_bits, count_bits)
    here = lax.axis_index("rcv").astype(jnp.int32).reshape(1)
    first_offset = partners[0, 0]
    first_far = first_offset >> low_bits - 1 & 1
    near_offset = jnp.where(first_far == 1, partners[1, 0], first_offset)
    far_index = (1 - first_far).reshape(1)

    near_in, far_in = route_high(predictions, predictions, near_offset, low_bits, count_bits)
    own, far_return, near_return = meet_both(
        near_in, far_in, predictions, observed, near_offset, far_index, low_bits, count_bits
    )
    near_return, far_return = route_high(near_return, far_return, near_offset, low_bits, count_bits)

    groups = stage_groups(count_bits)
    parts = partial_gradient(
        here, own, far_return, near_return, green_block, xor_order(groups), 1 << groups[0][1]
    )
    return scatter_sum(parts, groups)


def solution(mesh):
    placed = (P("rcv", None), P(None, "rcv", None), P(), P("rcv", None))
    return jax.shard_map(
        shards, mesh=mesh, in_specs=placed, out_specs=P("rcv", None), check_vma=False
    )
```

```python
import functools

import jax
import jax.numpy as jnp
from jax import lax
from jax.experimental import pallas as pl
from jax.experimental.pallas import tpu as pltpu
from jax.sharding import PartitionSpec as P

student_nu = 0.01
direct_bits = 5
chunk_rows = 256
block_rows = 1024
turn_rows = 128
f32 = jnp.float32


def send(value, offset):
    if offset == 0:
        return value
    return lax.ppermute(value, "rcv", [(i, i ^ offset) for i in range(lax.axis_size("rcv"))])


def is_mixed(device, top):
    return (device >> top ^ device >> top - 1) & 1 == 1


def send_mixed(value, mixed_offset, other_offset, top):
    pairs = [
        (i, i ^ (mixed_offset if is_mixed(i, top) else other_offset))
        for i in range(lax.axis_size("rcv"))
    ]
    return lax.ppermute(value, "rcv", pairs)


def contract_last(left, right):
    return lax.dot_general(left, right, (((1,), (1,)), ((), ())), preferred_element_type=f32)


def turn_kernel(rows_ref, turned_ref):
    turned_ref[...] = rows_ref[...].T


def turn(value):
    rows, samples = value.shape
    return pl.pallas_call(
        turn_kernel,
        out_shape=jax.ShapeDtypeStruct((samples, rows), value.dtype),
        grid=(rows // turn_rows,),
        in_specs=[pl.BlockSpec((turn_rows, samples), lambda c: (c, 0))],
        out_specs=pl.BlockSpec((samples, turn_rows), lambda c: (0, c)),
        compiler_params=pltpu.CompilerParams(dimension_semantics=("arbitrary",)),
    )(value)


def weights_of(gram, tile_obs, samples):
    residual = gram - tile_obs.astype(f32) * samples
    weights = ((student_nu + 1.0) * samples) * residual
    weights = weights / (student_nu * samples * samples + residual * residual)
    return weights.astype(jnp.bfloat16)


def pair_kernel(
    far_steps, _, mine_ref, mine_t, far_ref, near_ref, odd_obs, even_obs,
    far_back, near_back, even_weights, odd_weights, odd_gram, held_weights,
):
    step = pl.program_id(0)
    samples = mine_ref.shape[1]
    rows = jnp.where(step < far_steps, far_ref[...], near_ref[...])
    back_even = jnp.dot(mine_t[...], held_weights[...], preferred_element_type=f32)
    odd = weights_of(odd_gram[...], odd_obs[...], samples)
    even_gram = contract_last(mine_ref[...], rows[:chunk_rows])
    odd_weights[...] = odd
    back_odd = jnp.dot(mine_t[...], odd, preferred_element_type=f32)
    even = weights_of(even_gram, even_obs[...], samples)
    even_weights[...] = even
    held_weights[...] = even
    odd_gram[...] = contract_last(mine_ref[...], rows[chunk_rows:])
    back_even = (back_even * (1.0 / samples)).astype(jnp.bfloat16)
    back_odd = (back_odd * (1.0 / samples)).astype(jnp.bfloat16)

    @pl.when(step <= far_steps)
    def _():
        far_back[:, :chunk_rows] = back_even
        far_back[:, chunk_rows:] = back_odd

    @pl.when(step > far_steps)
    def _():
        near_back[:, :chunk_rows] = back_even
        near_back[:, chunk_rows:] = back_odd


def pair_products(mine, mine_t, far_rows, near_rows, observed, far_index):
    rows, samples = mine.shape
    chunks = rows // chunk_rows
    steps = rows // (2 * chunk_rows)
    double = 2 * chunk_rows

    def rows_at(first):
        return lambda s, far: (jnp.clip(s - first, 0, steps - 1), 0)

    def back_at(first):
        return lambda s, far: (0, jnp.clip(s - first, 0, steps - 1))

    def observed_at(shift):
        def at(s, far):
            chunk = jnp.clip(2 * s + shift, 0, 2 * chunks - 1)
            later = chunk >= chunks
            return jnp.where(later, 1 - far[0], far[0]), 0, jnp.where(later, chunk - chunks, chunk)

        return at

    tile = (None, rows, chunk_rows)
    back = jax.ShapeDtypeStruct((samples, rows), jnp.bfloat16)
    weights = jax.ShapeDtypeStruct((rows, (2 * steps + 1) * chunk_rows), jnp.bfloat16)
    return pl.pallas_call(
        functools.partial(pair_kernel, steps),
        out_shape=(back, back, weights, weights),
        grid_spec=pltpu.PrefetchScalarGridSpec(
            num_scalar_prefetch=1,
            grid=(2 * steps + 1,),
            in_specs=[
                pl.BlockSpec((rows, samples), lambda s, far: (0, 0)),
                pl.BlockSpec((samples, rows), lambda s, far: (0, 0)),
                pl.BlockSpec((double, samples), rows_at(0)),
                pl.BlockSpec((double, samples), rows_at(steps)),
                pl.BlockSpec(tile, observed_at(-1)),
                pl.BlockSpec(tile, observed_at(0)),
            ],
            out_specs=[
                pl.BlockSpec((samples, double), back_at(1)),
                pl.BlockSpec((samples, double), back_at(steps + 1)),
                pl.BlockSpec((rows, chunk_rows), lambda s, far: (0, s)),
                pl.BlockSpec((rows, chunk_rows), lambda s, far: (0, s)),
            ],
            scratch_shapes=[
                pltpu.VMEM((rows, chunk_rows), f32),
                pltpu.VMEM((rows, chunk_rows), jnp.bfloat16),
            ],
        ),
        compiler_params=pltpu.CompilerParams(dimension_semantics=("arbitrary",)),
    )(far_index, mine, mine_t, far_rows, near_rows, observed, observed)


def own_kernel(far_steps, far_ref, near_ref, even_weights, odd_weights, own_ref, total):
    step = pl.program_id(1)
    rows = jnp.where(step < far_steps, far_ref[...], near_ref[...])
    own = jnp.dot(even_weights[...], rows[:chunk_rows], preferred_element_type=f32)
    own += jnp.dot(odd_weights[...], rows[chunk_rows:], preferred_element_type=f32)
    total[...] = jnp.where(step == 0, own, total[...] + own)

    @pl.when(step == pl.num_programs(1) - 1)
    def _():
        own_ref[...] = (total[...] * (1.0 / far_ref.shape[1])).T


def own_product(far, near, even_weights, odd_weights):
    rows, samples = far.shape
    steps = rows // (2 * chunk_rows)
    double = 2 * chunk_rows
    return pl.pallas_call(
        functools.partial(own_kernel, steps),
        out_shape=jax.ShapeDtypeStruct((samples, rows), f32),
        grid=(rows // chunk_rows, 2 * steps),
        in_specs=[
            pl.BlockSpec((double, samples), lambda c, s: (jnp.clip(s, 0, steps - 1), 0)),
            pl.BlockSpec((double, samples), lambda c, s: (jnp.clip(s - steps, 0, steps - 1), 0)),
            pl.BlockSpec((chunk_rows, chunk_rows), lambda c, s: (c, s)),
            pl.BlockSpec((chunk_rows, chunk_rows), lambda c, s: (c, s + 1)),
        ],
        out_specs=pl.BlockSpec((samples, chunk_rows), lambda c, s: (0, c)),
        scratch_shapes=[pltpu.VMEM((chunk_rows, samples), f32)],
        compiler_params=pltpu.CompilerParams(dimension_semantics=("arbitrary", "arbitrary")),
    )(far, near, even_weights, odd_weights)


def partial_kernel(order, here_ref, own, far, near, green, *refs):
    outs, (own_in, far_in, near_in, green_in, total, turned, sems) = refs[:-7], refs[-7:]
    chunks = own.shape[1] // chunk_rows
    copies = []
    for chunk in range(chunks):
        columns = pl.ds(chunk * chunk_rows, chunk_rows)
        moves = [(own, own_in), (far, far_in), (near, near_in)]
        views = [(source.at[:, columns], held.at[:, columns]) for source, held in moves]
        views.append((green.at[columns], green_in.at[columns]))
        copies.append(
            [
                pltpu.make_async_copy(source, held, sems.at[chunk, place])
                for place, (source, held) in enumerate(views)
            ]
        )
    for batch in copies:
        for copy in batch:
            copy.start()
    for chunk, batch in enumerate(copies):
        for copy in batch:
            copy.wait()
        columns = slice(chunk * chunk_rows, (chunk + 1) * chunk_rows)
        adjoint = own_in[:, columns] + far_in[:, columns].astype(f32)
        adjoint = (adjoint + near_in[:, columns].astype(f32)).astype(jnp.bfloat16)
        product = jnp.dot(adjoint, green_in[columns], preferred_element_type=f32)
        total[...] = product if chunk == 0 else total[...] + product
    turned[...] = total[...].T
    block = turned.shape[0] // len(order)
    each = len(order) // len(outs)
    for place, index in enumerate(order):
        source = pl.multiple_of((here_ref[0] ^ index) * block, block)
        spot = place % each * block
        outs[place // each][spot : spot + block, :] = turned[pl.ds(source, block), :]


def partial_gradient(here, own, far_return, near_return, green_block, order, parts):
    samples, rows = own.shape
    cells = green_block.shape[1]
    natural = cells // len(order) % 8 != 0
    kernel_order, kernel_parts = ([0], 1) if natural else (order, parts)
    size = cells // kernel_parts
    outs = pl.pallas_call(
        functools.partial(partial_kernel, kernel_order),
        out_shape=[jax.ShapeDtypeStruct((size, samples), f32)] * kernel_parts,
        in_specs=[pl.BlockSpec(memory_space=pltpu.SMEM)]
        + [pl.BlockSpec(memory_space=pltpu.HBM)] * 4,
        out_specs=[pl.BlockSpec(memory_space=pltpu.VMEM)] * kernel_parts,
        scratch_shapes=[
            pltpu.VMEM((samples, rows), f32),
            pltpu.VMEM((samples, rows), jnp.bfloat16),
            pltpu.VMEM((samples, rows), jnp.bfloat16),
            pltpu.VMEM((rows, cells), jnp.bfloat16),
            pltpu.VMEM((samples, cells), f32),
            pltpu.VMEM((cells, samples), f32),
            pltpu.SemaphoreType.DMA((rows // chunk_rows, 4)),
        ],
    )(here * 0 if natural else here, own, far_return, near_return, green_block)
    if natural:
        blocks = outs[0].reshape(len(order), cells // len(order), samples)
        wanted = jnp.bitwise_xor(jnp.array(order, jnp.int32), here)
        blocks = jnp.take(blocks, wanted, axis=0).reshape(parts, cells // parts, samples)
        outs = [blocks[part] for part in range(parts)]
    return list(outs)


def route_high(near, far, near_offset, low_bits, count_bits):
    for level in range(low_bits, count_bits):
        takes_near = near_offset >> level & 1 == 1
        moved = send(jnp.where(takes_near, near, far), 1 << level)
        near = jnp.where(takes_near, moved, near)
        far = jnp.where(takes_near, far, moved)
    return near, far


def back_kernel(_, mine_ref, mine_t, other_ref, obs_ref, back_ref, weights_ref, *scratch):
    block, last = pl.program_id(1), pl.num_programs(1) - 1
    samples = mine_ref.shape[1]
    gram = contract_last(mine_ref[...], other_ref[...])
    weights = weights_of(gram, obs_ref[...], samples)
    weights_ref[...] = weights
    back = jnp.dot(mine_t[...], weights, preferred_element_type=f32)
    if not scratch:
        back_ref[...] = (back * (1.0 / samples)).astype(jnp.bfloat16)
        return
    (total,) = scratch
    back = jnp.where(block == 0, back, total[...] + back)
    total[...] = back

    @pl.when(block == last)
    def _():
        back_ref[...] = (back * (1.0 / samples)).astype(jnp.bfloat16)


def back_product(mine, mine_t, other, observed, meeting):
    rows, samples = mine.shape
    blocks = rows // block_rows
    return pl.pallas_call(
        back_kernel,
        out_shape=(
            jax.ShapeDtypeStruct((samples, rows), jnp.bfloat16),
            jax.ShapeDtypeStruct((rows, rows), jnp.bfloat16),
        ),
        grid_spec=pltpu.PrefetchScalarGridSpec(
            num_scalar_prefetch=1,
            grid=(rows // chunk_rows, blocks),
            in_specs=[
                pl.BlockSpec((block_rows, samples), lambda c, r, meeting: (r, 0)),
                pl.BlockSpec((samples, block_rows), lambda c, r, meeting: (0, r)),
                pl.BlockSpec((chunk_rows, samples), lambda c, r, meeting: (c, 0)),
                pl.BlockSpec(
                    (None, block_rows, chunk_rows), lambda c, r, meeting: (meeting[0], r, c)
                ),
            ],
            out_specs=[
                pl.BlockSpec((samples, chunk_rows), lambda c, r, meeting: (0, c)),
                pl.BlockSpec((block_rows, chunk_rows), lambda c, r, meeting: (r, c)),
            ],
            scratch_shapes=[pltpu.VMEM((samples, chunk_rows), f32)] if blocks > 1 else [],
        ),
        compiler_params=pltpu.CompilerParams(dimension_semantics=("arbitrary", "arbitrary")),
    )(meeting, mine, mine_t, other, observed)


def total_kernel(first_ref, second_ref, first_weights, second_weights, own_ref, total):
    step = pl.program_id(1)
    own = jnp.dot(first_weights[...], first_ref[...], preferred_element_type=f32)
    own += jnp.dot(second_weights[...], second_ref[...], preferred_element_type=f32)
    total[...] = jnp.where(step == 0, own, total[...] + own)

    @pl.when(step == pl.num_programs(1) - 1)
    def _():
        own_ref[...] = (total[...] * (1.0 / first_ref.shape[1])).T


def own_total(first, second, first_weights, second_weights):
    rows, samples = first.shape
    values = pl.BlockSpec((chunk_rows, samples), lambda c, s: (s, 0))
    weights = pl.BlockSpec((chunk_rows, chunk_rows), lambda c, s: (c, s))
    return pl.pallas_call(
        total_kernel,
        out_shape=jax.ShapeDtypeStruct((samples, rows), f32),
        grid=(rows // chunk_rows, rows // chunk_rows),
        in_specs=[values, values, weights, weights],
        out_specs=pl.BlockSpec((samples, chunk_rows), lambda c, s: (0, c)),
        scratch_shapes=[pltpu.VMEM((chunk_rows, samples), f32)],
        compiler_params=pltpu.CompilerParams(dimension_semantics=("arbitrary", "arbitrary")),
    )(first, second, first_weights, second_weights)


def meet_apart(near, far, mine, observed, far_index, low_offset, low_bits, lowest):
    mask = (1 << low_bits) - 1
    offsets = range(lowest, 1 << low_bits - 2)

    def arrive(offset):
        def run(near, far, mine):
            far_rows = send(far, offset ^ mask)
            return far_rows, send(near, offset), turn(mine)

        return run

    def leave(offset):
        def run(far_rows, near_rows, far_back, near_back, *weights):
            far_return = send(far_back, offset ^ mask)
            near_return = send(near_back, offset)
            return own_product(far_rows, near_rows, *weights), far_return, near_return

        return run

    chosen = low_offset - lowest
    far_rows, near_rows, mine_t = lax.switch(
        chosen, [arrive(offset) for offset in offsets], near, far, mine
    )
    products = pair_products(mine, mine_t, far_rows, near_rows, observed, far_index)
    return lax.switch(
        chosen, [leave(offset) for offset in offsets], far_rows, near_rows, *products
    )


def meet_mixed(near, far, mine, observed, far_index, low_offset, low_bits):
    mask = (1 << low_bits) - 1
    top = low_bits - 1
    lowest = 1 << top - 1
    mixed = is_mixed(lax.axis_index("rcv"), top)

    def branch(offset):
        close, apart = offset, offset ^ mask

        def run(near, far, mine, observed, first_meeting):
            first_out = near if near is far else jnp.where(mixed, near, far)
            second_out = near if near is far else jnp.where(mixed, far, near)
            first = send_mixed(first_out, close, apart, top)
            second = send_mixed(second_out, apart, close, top)
            mine_t = turn(mine)
            back, first_weights = back_product(mine, mine_t, first, observed, first_meeting)
            first_return = send_mixed(back, apart, close, top)
            back, second_weights = back_product(mine, mine_t, second, observed, 1 - first_meeting)
            second_return = send_mixed(back, close, apart, top)
            own = own_total(first, second, first_weights, second_weights)
            return own, first_return, second_return

        return run

    first_meeting = jnp.where(mixed, far_index, 1 - far_index)
    if near is far:
        one = lambda run: lambda rows, *rest: run(rows, rows, *rest)
        branches = [one(branch(offset)) for offset in range(lowest, 1 << top)]
        return lax.switch(low_offset - lowest, branches, near, mine, observed, first_meeting)
    branches = [branch(offset) for offset in range(lowest, 1 << top)]
    own, first_return, second_return = lax.switch(
        low_offset - lowest, branches, near, far, mine, observed, first_meeting
    )
    return (
        own,
        jnp.where(mixed, second_return, first_return),
        jnp.where(mixed, first_return, second_return),
    )


def meet_both(near, far, mine, observed, near_offset, far_index, low_bits, count_bits):
    low_offset = near_offset & (1 << low_bits) - 1
    lowest = 1 if low_bits == count_bits else 0

    def with_inputs(meet, *more):
        if near is far:
            return lambda rows, *rest: meet(rows, rows, *rest, *more)
        return lambda near, far, *rest: meet(near, far, *rest, *more)

    inputs = (near,) if near is far else (near, far)
    return lax.cond(
        low_offset >> low_bits - 2 & 1 == 1,
        with_inputs(meet_mixed, low_bits),
        with_inputs(meet_apart, low_bits, lowest),
        *inputs,
        mine,
        observed,
        far_index,
        low_offset,
    )


def stage_groups(count_bits):
    groups, level = [], 0
    while level < count_bits:
        width = min(1 if level == 0 else 2, count_bits - level)
        groups.append((level, width))
        level += width
    return groups


def xor_order(groups):
    order = [0]
    for level, width in groups:
        order = [block | digit << level for block in order for digit in range(1 << width)]
    return order


def scatter_sum(parts, groups):
    total = None
    for stage, (level, width) in enumerate(groups):
        if total is not None:
            size = total.shape[0] >> width
            parts = [total[digit * size : (digit + 1) * size] for digit in range(1 << width)]
        kind = jnp.bfloat16 if stage == 1 else f32
        moved = [
            send(parts[digit].astype(kind), digit << level) for digit in range(1, 1 << width)
        ]
        total = parts[0]
        for piece in moved:
            total = total + piece.astype(f32)
    return total


def shards(predictions, observed, partners, green_block):
    count_bits = lax.axis_size("rcv").bit_length() - 1
    low_bits = min(direct_bits, count_bits)
    here = lax.axis_index("rcv").astype(jnp.int32).reshape(1)
    first_offset = partners[0, 0]
    first_far = first_offset >> low_bits - 1 & 1
    near_offset = jnp.where(first_far == 1, partners[1, 0], first_offset)
    far_index = (1 - first_far).reshape(1)

    near_in, far_in = route_high(predictions, predictions, near_offset, low_bits, count_bits)
    own, far_return, near_return = meet_both(
        near_in, far_in, predictions, observed, near_offset, far_index, low_bits, count_bits
    )
    near_return, far_return = route_high(near_return, far_return, near_offset, low_bits, count_bits)

    groups = stage_groups(count_bits)
    parts = partial_gradient(
        here, own, far_return, near_return, green_block, xor_order(groups), 1 << groups[0][1]
    )
    return scatter_sum(parts, groups)


def solution(mesh):
    placed = (P("rcv", None), P(None, "rcv", None), P(), P("rcv", None))
    return jax.shard_map(
        shards, mesh=mesh, in_specs=placed, out_specs=P("rcv", None), check_vma=False
    )
```

```python
import functools

import jax
import jax.numpy as jnp
from jax import lax
from jax.experimental import pallas as pl
from jax.experimental.pallas import tpu as pltpu
from jax.sharding import PartitionSpec as P

student_nu = 0.01
direct_bits = 5
chunk_rows = 256
block_rows = 512
turn_rows = 128
f32 = jnp.float32


def send(value, offset):
    if offset == 0:
        return value
    return lax.ppermute(value, "rcv", [(i, i ^ offset) for i in range(lax.axis_size("rcv"))])


def is_mixed(device, top):
    return (device >> top ^ device >> top - 1) & 1 == 1


def send_mixed(value, mixed_offset, other_offset, top):
    pairs = [
        (i, i ^ (mixed_offset if is_mixed(i, top) else other_offset))
        for i in range(lax.axis_size("rcv"))
    ]
    return lax.ppermute(value, "rcv", pairs)


def contract_last(left, right):
    return lax.dot_general(left, right, (((1,), (1,)), ((), ())), preferred_element_type=f32)


def turn_kernel(rows_ref, turned_ref):
    turned_ref[...] = rows_ref[...].T


def turn(value):
    rows, samples = value.shape
    return pl.pallas_call(
        turn_kernel,
        out_shape=jax.ShapeDtypeStruct((samples, rows), value.dtype),
        grid=(rows // turn_rows,),
        in_specs=[pl.BlockSpec((turn_rows, samples), lambda c: (c, 0))],
        out_specs=pl.BlockSpec((samples, turn_rows), lambda c: (0, c)),
        compiler_params=pltpu.CompilerParams(dimension_semantics=("arbitrary",)),
    )(value)


def weights_of(gram, tile_obs, samples):
    residual = gram - tile_obs.astype(f32) * samples
    weights = ((student_nu + 1.0) * samples) * residual
    weights = weights / (student_nu * samples * samples + residual * residual)
    return weights.astype(jnp.bfloat16)


def pair_kernel(
    far_steps, _, mine_ref, mine_t, far_ref, near_ref, odd_obs, even_obs,
    far_back, near_back, even_weights, odd_weights, odd_gram, held_weights,
):
    step = pl.program_id(0)
    samples = mine_ref.shape[1]
    rows = jnp.where(step < far_steps, far_ref[...], near_ref[...])
    back_even = jnp.dot(mine_t[...], held_weights[...], preferred_element_type=f32)
    odd = weights_of(odd_gram[...], odd_obs[...], samples)
    even_gram = contract_last(mine_ref[...], rows[:chunk_rows])
    odd_weights[...] = odd
    back_odd = jnp.dot(mine_t[...], odd, preferred_element_type=f32)
    even = weights_of(even_gram, even_obs[...], samples)
    even_weights[...] = even
    held_weights[...] = even
    odd_gram[...] = contract_last(mine_ref[...], rows[chunk_rows:])
    back_even = (back_even * (1.0 / samples)).astype(jnp.bfloat16)
    back_odd = (back_odd * (1.0 / samples)).astype(jnp.bfloat16)

    @pl.when(step <= far_steps)
    def _():
        far_back[:, :chunk_rows] = back_even
        far_back[:, chunk_rows:] = back_odd

    @pl.when(step > far_steps)
    def _():
        near_back[:, :chunk_rows] = back_even
        near_back[:, chunk_rows:] = back_odd


def pair_products(mine, mine_t, far_rows, near_rows, observed, far_index):
    rows, samples = mine.shape
    chunks = rows // chunk_rows
    steps = rows // (2 * chunk_rows)
    double = 2 * chunk_rows

    def rows_at(first):
        return lambda s, far: (jnp.clip(s - first, 0, steps - 1), 0)

    def back_at(first):
        return lambda s, far: (0, jnp.clip(s - first, 0, steps - 1))

    def observed_at(shift):
        def at(s, far):
            chunk = jnp.clip(2 * s + shift, 0, 2 * chunks - 1)
            later = chunk >= chunks
            return jnp.where(later, 1 - far[0], far[0]), 0, jnp.where(later, chunk - chunks, chunk)

        return at

    tile = (None, rows, chunk_rows)
    back = jax.ShapeDtypeStruct((samples, rows), jnp.bfloat16)
    weights = jax.ShapeDtypeStruct((rows, (2 * steps + 1) * chunk_rows), jnp.bfloat16)
    return pl.pallas_call(
        functools.partial(pair_kernel, steps),
        out_shape=(back, back, weights, weights),
        grid_spec=pltpu.PrefetchScalarGridSpec(
            num_scalar_prefetch=1,
            grid=(2 * steps + 1,),
            in_specs=[
                pl.BlockSpec((rows, samples), lambda s, far: (0, 0)),
                pl.BlockSpec((samples, rows), lambda s, far: (0, 0)),
                pl.BlockSpec((double, samples), rows_at(0)),
                pl.BlockSpec((double, samples), rows_at(steps)),
                pl.BlockSpec(tile, observed_at(-1)),
                pl.BlockSpec(tile, observed_at(0)),
            ],
            out_specs=[
                pl.BlockSpec((samples, double), back_at(1)),
                pl.BlockSpec((samples, double), back_at(steps + 1)),
                pl.BlockSpec((rows, chunk_rows), lambda s, far: (0, s)),
                pl.BlockSpec((rows, chunk_rows), lambda s, far: (0, s)),
            ],
            scratch_shapes=[
                pltpu.VMEM((rows, chunk_rows), f32),
                pltpu.VMEM((rows, chunk_rows), jnp.bfloat16),
            ],
        ),
        compiler_params=pltpu.CompilerParams(dimension_semantics=("arbitrary",)),
    )(far_index, mine, mine_t, far_rows, near_rows, observed, observed)


def own_kernel(far_steps, far_ref, near_ref, even_weights, odd_weights, own_ref, total):
    step = pl.program_id(1)
    rows = jnp.where(step < far_steps, far_ref[...], near_ref[...])
    own = jnp.dot(even_weights[...], rows[:chunk_rows], preferred_element_type=f32)
    own += jnp.dot(odd_weights[...], rows[chunk_rows:], preferred_element_type=f32)
    total[...] = jnp.where(step == 0, own, total[...] + own)

    @pl.when(step == pl.num_programs(1) - 1)
    def _():
        own_ref[...] = (total[...] * (1.0 / far_ref.shape[1])).T


def own_product(far, near, even_weights, odd_weights):
    rows, samples = far.shape
    steps = rows // (2 * chunk_rows)
    double = 2 * chunk_rows
    return pl.pallas_call(
        functools.partial(own_kernel, steps),
        out_shape=pltpu.HBM((samples, rows), f32),
        grid=(rows // chunk_rows, 2 * steps),
        in_specs=[
            pl.BlockSpec((double, samples), lambda c, s: (jnp.clip(s, 0, steps - 1), 0)),
            pl.BlockSpec((double, samples), lambda c, s: (jnp.clip(s - steps, 0, steps - 1), 0)),
            pl.BlockSpec((chunk_rows, chunk_rows), lambda c, s: (c, s)),
            pl.BlockSpec((chunk_rows, chunk_rows), lambda c, s: (c, s + 1)),
        ],
        out_specs=pl.BlockSpec((samples, chunk_rows), lambda c, s: (0, c)),
        scratch_shapes=[pltpu.VMEM((chunk_rows, samples), f32)],
        compiler_params=pltpu.CompilerParams(dimension_semantics=("arbitrary", "arbitrary")),
    )(far, near, even_weights, odd_weights)


def partial_kernel(order, here_ref, own, far, near, green, *refs):
    outs, (own_in, far_in, near_in, green_in, total, turned, sems) = refs[:-7], refs[-7:]
    chunks = own.shape[1] // chunk_rows
    copies = []
    for chunk in range(chunks):
        columns = pl.ds(chunk * chunk_rows, chunk_rows)
        moves = [(own, own_in), (far, far_in), (near, near_in)]
        views = [(source.at[:, columns], held.at[:, columns]) for source, held in moves]
        views.append((green.at[columns], green_in.at[columns]))
        copies.append(
            [
                pltpu.make_async_copy(source, held, sems.at[chunk, place])
                for place, (source, held) in enumerate(views)
            ]
        )
    for batch in copies:
        for copy in batch:
            copy.start()
    for chunk, batch in enumerate(copies):
        for copy in batch:
            copy.wait()
        columns = slice(chunk * chunk_rows, (chunk + 1) * chunk_rows)
        adjoint = own_in[:, columns] + far_in[:, columns].astype(f32)
        adjoint = (adjoint + near_in[:, columns].astype(f32)).astype(jnp.bfloat16)
        product = jnp.dot(adjoint, green_in[columns], preferred_element_type=f32)
        total[...] = product if chunk == 0 else total[...] + product
    turned[...] = total[...].T
    block = turned.shape[0] // len(order)
    each = len(order) // len(outs)
    for place, index in enumerate(order):
        source = pl.multiple_of((here_ref[0] ^ index) * block, block)
        spot = place % each * block
        outs[place // each][spot : spot + block, :] = turned[pl.ds(source, block), :]


def partial_gradient(here, own, far_return, near_return, green_block, order, parts):
    samples, rows = own.shape
    cells = green_block.shape[1]
    natural = cells // len(order) % 8 != 0
    kernel_order, kernel_parts = ([0], 1) if natural else (order, parts)
    size = cells // kernel_parts
    outs = pl.pallas_call(
        functools.partial(partial_kernel, kernel_order),
        out_shape=[pltpu.VMEM((size, samples), f32)] * kernel_parts,
        in_specs=[pl.BlockSpec(memory_space=pltpu.SMEM)]
        + [pl.BlockSpec(memory_space=pltpu.HBM)] * 4,
        out_specs=[pl.BlockSpec(memory_space=pltpu.VMEM)] * kernel_parts,
        scratch_shapes=[
            pltpu.VMEM((samples, rows), f32),
            pltpu.VMEM((samples, rows), jnp.bfloat16),
            pltpu.VMEM((samples, rows), jnp.bfloat16),
            pltpu.VMEM((rows, cells), jnp.bfloat16),
            pltpu.VMEM((samples, cells), f32),
            pltpu.VMEM((cells, samples), f32),
            pltpu.SemaphoreType.DMA((rows // chunk_rows, 4)),
        ],
    )(here * 0 if natural else here, own, far_return, near_return, green_block)
    if natural:
        blocks = outs[0].reshape(len(order), cells // len(order), samples)
        wanted = jnp.bitwise_xor(jnp.array(order, jnp.int32), here)
        blocks = jnp.take(blocks, wanted, axis=0).reshape(parts, cells // parts, samples)
        outs = [blocks[part] for part in range(parts)]
    return list(outs)


def route_high(near, far, near_offset, low_bits, count_bits):
    for level in range(low_bits, count_bits):
        takes_near = near_offset >> level & 1 == 1
        moved = send(jnp.where(takes_near, near, far), 1 << level)
        near = jnp.where(takes_near, moved, near)
        far = jnp.where(takes_near, far, moved)
    return near, far


def back_kernel(_, mine_ref, mine_t, other_ref, obs_ref, back_ref, weights_ref, *scratch):
    block, last = pl.program_id(1), pl.num_programs(1) - 1
    samples = mine_ref.shape[1]
    gram = contract_last(mine_ref[...], other_ref[...])
    weights = weights_of(gram, obs_ref[...], samples)
    weights_ref[...] = weights
    back = jnp.dot(mine_t[...], weights, preferred_element_type=f32)
    if not scratch:
        back_ref[...] = (back * (1.0 / samples)).astype(jnp.bfloat16)
        return
    (total,) = scratch
    back = jnp.where(block == 0, back, total[...] + back)
    total[...] = back

    @pl.when(block == last)
    def _():
        back_ref[...] = (back * (1.0 / samples)).astype(jnp.bfloat16)


def back_product(mine, mine_t, other, observed, meeting):
    rows, samples = mine.shape
    blocks = rows // block_rows
    return pl.pallas_call(
        back_kernel,
        out_shape=(
            jax.ShapeDtypeStruct((samples, rows), jnp.bfloat16),
            jax.ShapeDtypeStruct((rows, rows), jnp.bfloat16),
        ),
        grid_spec=pltpu.PrefetchScalarGridSpec(
            num_scalar_prefetch=1,
            grid=(rows // chunk_rows, blocks),
            in_specs=[
                pl.BlockSpec((block_rows, samples), lambda c, r, meeting: (r, 0)),
                pl.BlockSpec((samples, block_rows), lambda c, r, meeting: (0, r)),
                pl.BlockSpec((chunk_rows, samples), lambda c, r, meeting: (c, 0)),
                pl.BlockSpec(
                    (None, block_rows, chunk_rows), lambda c, r, meeting: (meeting[0], r, c)
                ),
            ],
            out_specs=[
                pl.BlockSpec((samples, chunk_rows), lambda c, r, meeting: (0, c)),
                pl.BlockSpec((block_rows, chunk_rows), lambda c, r, meeting: (r, c)),
            ],
            scratch_shapes=[pltpu.VMEM((samples, chunk_rows), f32)] if blocks > 1 else [],
        ),
        compiler_params=pltpu.CompilerParams(dimension_semantics=("arbitrary", "arbitrary")),
    )(meeting, mine, mine_t, other, observed)


def total_kernel(first_ref, second_ref, first_weights, second_weights, own_ref, total):
    step = pl.program_id(1)
    own = jnp.dot(first_weights[...], first_ref[...], preferred_element_type=f32)
    own += jnp.dot(second_weights[...], second_ref[...], preferred_element_type=f32)
    total[...] = jnp.where(step == 0, own, total[...] + own)

    @pl.when(step == pl.num_programs(1) - 1)
    def _():
        own_ref[...] = (total[...] * (1.0 / first_ref.shape[1])).T


def own_total(first, second, first_weights, second_weights):
    rows, samples = first.shape
    values = pl.BlockSpec((chunk_rows, samples), lambda c, s: (s, 0))
    weights = pl.BlockSpec((chunk_rows, chunk_rows), lambda c, s: (c, s))
    return pl.pallas_call(
        total_kernel,
        out_shape=pltpu.HBM((samples, rows), f32),
        grid=(rows // chunk_rows, rows // chunk_rows),
        in_specs=[values, values, weights, weights],
        out_specs=pl.BlockSpec((samples, chunk_rows), lambda c, s: (0, c)),
        scratch_shapes=[pltpu.VMEM((chunk_rows, samples), f32)],
        compiler_params=pltpu.CompilerParams(dimension_semantics=("arbitrary", "arbitrary")),
    )(first, second, first_weights, second_weights)


def meet_apart(near, far, mine, observed, far_index, low_offset, low_bits, lowest):
    mask = (1 << low_bits) - 1
    offsets = range(lowest, 1 << low_bits - 2)

    def arrive(offset):
        def run(near, far, mine):
            far_rows = send(far, offset ^ mask)
            return far_rows, send(near, offset), turn(mine)

        return run

    def leave(offset):
        def run(far_rows, near_rows, far_back, near_back, *weights):
            far_return = send(far_back, offset ^ mask)
            near_return = send(near_back, offset)
            return own_product(far_rows, near_rows, *weights), far_return, near_return

        return run

    chosen = low_offset - lowest
    far_rows, near_rows, mine_t = lax.switch(
        chosen, [arrive(offset) for offset in offsets], near, far, mine
    )
    products = pair_products(mine, mine_t, far_rows, near_rows, observed, far_index)
    return lax.switch(
        chosen, [leave(offset) for offset in offsets], far_rows, near_rows, *products
    )


def meet_mixed(near, far, mine, observed, far_index, low_offset, low_bits):
    mask = (1 << low_bits) - 1
    top = low_bits - 1
    lowest = 1 << top - 1
    mixed = is_mixed(lax.axis_index("rcv"), top)

    def branch(offset):
        close, apart = offset, offset ^ mask

        def run(near, far, mine, observed, first_meeting):
            first_out = near if near is far else jnp.where(mixed, near, far)
            second_out = near if near is far else jnp.where(mixed, far, near)
            first = send_mixed(first_out, close, apart, top)
            second = send_mixed(second_out, apart, close, top)
            mine_t = turn(mine)
            back, first_weights = back_product(mine, mine_t, first, observed, first_meeting)
            first_return = send_mixed(back, apart, close, top)
            back, second_weights = back_product(mine, mine_t, second, observed, 1 - first_meeting)
            second_return = send_mixed(back, close, apart, top)
            own = own_total(first, second, first_weights, second_weights)
            return own, first_return, second_return

        return run

    first_meeting = jnp.where(mixed, far_index, 1 - far_index)
    if near is far:
        one = lambda run: lambda rows, *rest: run(rows, rows, *rest)
        branches = [one(branch(offset)) for offset in range(lowest, 1 << top)]
        return lax.switch(low_offset - lowest, branches, near, mine, observed, first_meeting)
    branches = [branch(offset) for offset in range(lowest, 1 << top)]
    own, first_return, second_return = lax.switch(
        low_offset - lowest, branches, near, far, mine, observed, first_meeting
    )
    return (
        own,
        jnp.where(mixed, second_return, first_return),
        jnp.where(mixed, first_return, second_return),
    )


def meet_both(near, far, mine, observed, near_offset, far_index, low_bits, count_bits):
    low_offset = near_offset & (1 << low_bits) - 1
    lowest = 1 if low_bits == count_bits else 0

    def with_inputs(meet, *more):
        if near is far:
            return lambda rows, *rest: meet(rows, rows, *rest, *more)
        return lambda near, far, *rest: meet(near, far, *rest, *more)

    inputs = (near,) if near is far else (near, far)
    return lax.cond(
        low_offset >> low_bits - 2 & 1 == 1,
        with_inputs(meet_mixed, low_bits),
        with_inputs(meet_apart, low_bits, lowest),
        *inputs,
        mine,
        observed,
        far_index,
        low_offset,
    )


def stage_groups(count_bits):
    groups, level = [], 0
    while level < count_bits:
        width = min(1 if level == 0 else 2, count_bits - level)
        groups.append((level, width))
        level += width
    return groups


def xor_order(groups):
    order = [0]
    for level, width in groups:
        order = [block | digit << level for block in order for digit in range(1 << width)]
    return order


def scatter_sum(parts, groups):
    total = None
    for stage, (level, width) in enumerate(groups):
        if total is not None:
            size = total.shape[0] >> width
            parts = [total[digit * size : (digit + 1) * size] for digit in range(1 << width)]
        kind = jnp.bfloat16 if stage == 1 else f32
        moved = [
            send(parts[digit].astype(kind), digit << level) for digit in range(1, 1 << width)
        ]
        total = parts[0]
        for piece in moved:
            total = total + piece.astype(f32)
    return total


def shards(predictions, observed, partners, green_block):
    count_bits = lax.axis_size("rcv").bit_length() - 1
    low_bits = min(direct_bits, count_bits)
    here = lax.axis_index("rcv").astype(jnp.int32).reshape(1)
    first_offset = partners[0, 0]
    first_far = first_offset >> low_bits - 1 & 1
    near_offset = jnp.where(first_far == 1, partners[1, 0], first_offset)
    far_index = (1 - first_far).reshape(1)

    near_in, far_in = route_high(predictions, predictions, near_offset, low_bits, count_bits)
    own, far_return, near_return = meet_both(
        near_in, far_in, predictions, observed, near_offset, far_index, low_bits, count_bits
    )
    near_return, far_return = route_high(near_return, far_return, near_offset, low_bits, count_bits)

    groups = stage_groups(count_bits)
    parts = partial_gradient(
        here, own, far_return, near_return, green_block, xor_order(groups), 1 << groups[0][1]
    )
    return scatter_sum(parts, groups)


def solution(mesh):
    placed = (P("rcv", None), P(None, "rcv", None), P(), P("rcv", None))
    return jax.shard_map(
        shards, mesh=mesh, in_specs=placed, out_specs=P("rcv", None), check_vma=False
    )
```
